768 devices in a mesh: elem: 96 (over y, x, z_lo), state: 8 (over z_hi, core).
Axes of the slice: x: 4, y: 8, z: 12 (z_hi: 4, z_lo: 3; z = z_hi * 3 + z_lo), core: 2. Of those that a mesh axis runs over, the one named last changes fastest.
Arguments:
- cell_matrices: bfloat16 [384, 512, 512], P('elem'), may hold values from -0.25 to 0.25
- initial_states: bfloat16 [384, 512, 1024], P('elem', None, 'state'), may hold values from -6 to 6
- face_map: int32 [384, 64], P('elem'), may hold values from 0 to 63, each once within a row
Outputs:
- filtered_states: bfloat16 [384, 512, 1024], P('elem', None, 'state')
- projected_hamiltonian: float32 [1024, 1024], P('state')
- projected_intersection: float32 [1024, 1024], P('state')
The draws below stay inside these ranges and needn't reach their ends.
Inputs may be any that keep to these rules, and one draw needn't show every extreme that they name: Each row of face_map is a permutation of 0 to 63.
All inputs are finite; a program needn't handle non-finite values.
Results may differ from the reference program's by a relative error of at most 0.013.
Values may be sent and summed in bfloat16 or wider, within the bound.
No kernel may reach another device: no remote copies, remote signals or barrier semaphores. Data moves between devices by JAX's collectives and lax.ppermute only.
A program may use at most 32 MiB of HBM per device.

```python
import jax
import jax.numpy as jnp
from jax import lax

ORB = 1024
PASSES = 4
NODES = 512
FACE = 64
CELLS = 384


def steps_of(own_key, dims, shards, least, high):
    def one(position, parts):
        heights = jax.random.uniform(jax.random.fold_in(jax.random.fold_in(own_key, 6), position), (parts,), jnp.float32, least / len(shards), high / len(shards))
        return jnp.repeat(jnp.exp(heights), dims[position] // parts).reshape((-1,) + (1,) * (len(dims) - position - 1))

    gain = one(*shards[0])
    for cut in shards[1:]:
        gain = gain * one(*cut)
    return gain


def gaussian(own_key, extent, deviation, bound, pieces=(), held_as=jnp.bfloat16):
    loudness = steps_of(own_key, extent, pieces, -0.22, 0.18) if pieces else 1.0
    result = jax.random.normal(own_key, extent, jnp.float32) * deviation * loudness
    return jnp.minimum(jnp.maximum(result, -bound), bound).astype(held_as)


def setup_inputs(seed: int = 0) -> dict:
    seeds = jax.random.split(jax.random.key(seed), 4)
    return {
        "cell_matrices": gaussian(seeds[0], (CELLS, NODES, NODES), NODES ** -0.5, 0.25, ((0, 96),)),
        "initial_states": gaussian(seeds[1], (CELLS, NODES, ORB), 1.0, 6.0, ((0, 96), (2, 8))),
        "face_map": jax.vmap(lambda own: jax.random.permutation(own, FACE))(jax.random.split(seeds[2], CELLS)).reshape((CELLS, FACE)).astype(jnp.int32),
    }


filter_width = 2.5


def apply_operator(cell_matrices, values, onehot):
    face = onehot.shape[1]
    orbitals = values.shape[2]
    products = jnp.einsum('cij,cjo->cio', cell_matrices.astype(jnp.float32), values.astype(jnp.float32))
    lower_face = products[:, :face]
    upper_face = products[:, -face:]
    middle = products[:, face:-face]
    to_next = jnp.einsum('cfm,cfo->cmo', onehot, upper_face, precision=lax.Precision.HIGHEST)
    zero_face = jnp.zeros((1, face, orbitals), jnp.float32)
    lower_next = jnp.concatenate([lower_face[1:], zero_face], 0)
    from_next = jnp.einsum('cfm,cmo->cfo', onehot, lower_next, precision=lax.Precision.HIGHEST)
    from_low = jnp.concatenate([zero_face, to_next[:-1]], 0)
    return jnp.concatenate([lower_face + from_low, middle, upper_face + from_next], 1)


def reference(cell_matrices, initial_states, face_map):
    face = face_map.shape[1]
    cells = cell_matrices.shape[0]
    nodes = cell_matrices.shape[1]
    onehot = (face_map[:, :, None] == jnp.arange(face, dtype=jnp.int32)[None, None, :]).astype(jnp.float32)
    previous = initial_states.astype(jnp.float32)
    current = previous
    current_b = initial_states
    for degree in range(PASSES):
        image = apply_operator(cell_matrices, current_b, onehot)
        if degree == 0:
            following = image / filter_width
        else:
            following = (2.0 / filter_width) * image - previous
        previous = current
        current = following
        current_b = following.astype(jnp.bfloat16)
    states = current_b
    image_b = apply_operator(cell_matrices, states, onehot).astype(jnp.bfloat16)
    has_next = jnp.arange(cells, dtype=jnp.int32) < cells - 1
    on_upper = jnp.arange(nodes, dtype=jnp.int32) >= nodes - face
    dropped = has_next[:, None] & on_upper[None, :]
    weighted = jnp.where(dropped[:, :, None], jnp.zeros((), jnp.bfloat16), states)
    flat_weighted = weighted.reshape(cells * nodes, -1)
    flat_image = image_b.reshape(cells * nodes, -1)
    inv_points = 1.0 / (cells * nodes)
    intersection = jnp.dot(flat_weighted.T, flat_weighted, preferred_element_type=jnp.float32) * inv_points
    hamiltonian = jnp.dot(flat_weighted.T, flat_image, preferred_element_type=jnp.float32) * inv_points
    return states, hamiltonian, intersection
```

```python
import jax
import jax.numpy as jnp
from jax import lax
from jax.experimental import pallas as pl
from jax.experimental.pallas import tpu as pltpu
from jax.sharding import Mesh
from jax.sharding import PartitionSpec as P

PASSES = 4
ELEM = (("y", 8), ("x", 4), ("zl", 3))
STATE = (("zh", 4), ("core", 2))


filter_width = 2.5

f32 = jnp.float32
bf16 = jnp.bfloat16
elem = tuple(name for name, _ in ELEM)
state = tuple(name for name, _ in STATE)


def dot(a, b, dims=((1,), (0,))):
    return lax.dot_general(a, b, (dims, ((), ())), preferred_element_type=f32)


def shifted(faces, up):
    count = lax.axis_size(elem)
    pairs = [(i, i + 1) if up else (i + 1, i) for i in range(count - 1)]
    return lax.ppermute(faces, elem, pairs)


def reorder_kernel(perm_ref, perm_t_ref, k_ref, out_ref):
    face = perm_t_ref.shape[1]
    nodes = k_ref.shape[1]
    wide = perm_ref.shape[1]
    out_ref[0, :, : nodes - wide] = k_ref[0, :, : nodes - wide]
    out_ref[0, :, nodes - wide :] = dot(k_ref[0, :, nodes - wide :], perm_ref[0]).astype(bf16)
    out_ref[0, nodes - face :, :] = dot(perm_t_ref[0], out_ref[0, nodes - face :, :]).astype(bf16)


def reordered(cell_matrices, onehot):
    cells, nodes = cell_matrices.shape[:2]
    face = onehot.shape[1]
    wide = 2 * face
    eye = jnp.broadcast_to(jnp.eye(face, dtype=bf16), (cells, face, face))
    none = jnp.zeros((cells, face, face), bf16)
    perm = jnp.concatenate(
        [jnp.concatenate([eye, none], 2), jnp.concatenate([none, onehot], 2)], 1
    )
    perm_t = jnp.swapaxes(onehot, 1, 2)
    return pl.pallas_call(
        reorder_kernel,
        grid=(cells,),
        in_specs=[
            pl.BlockSpec((1, wide, wide), lambda c: (c, 0, 0)),
            pl.BlockSpec((1, face, face), lambda c: (c, 0, 0)),
            pl.BlockSpec((1, nodes, nodes), lambda c: (c, 0, 0)),
        ],
        out_specs=pl.BlockSpec((1, nodes, nodes), lambda c: (c, 0, 0)),
        out_shape=jax.ShapeDtypeStruct(cell_matrices.shape, bf16),
        name="reorder",
    )(perm, perm_t, cell_matrices)


def scatter_rows(part, out_ref, block):
    xs, ys, _, rows, cols = out_ref.shape
    for x in range(xs):
        for y in range(ys):
            out_ref[x, y, block] = part[x * rows : (x + 1) * rows, y * cols : (y + 1) * cols].astype(bf16)


def gram_own_kernel(where_ref, k_ref, rows_ref, out_ref, right_ref):
    blocks, total, orb = rows_ref.shape
    nodes = k_ref.shape[1]
    face = total - nodes
    inner = nodes - face
    is_last = where_ref[1] == 1
    for s in range(blocks):
        at = slice(s * orb, (s + 1) * orb)
        right_ref[:, at] = dot(k_ref[0], rows_ref[s, :nodes]).astype(bf16)
        at = slice((blocks + s) * orb, (blocks + s + 1) * orb)
        right_ref[:inner, at] = rows_ref[s, :inner]
        paired = rows_ref[s, nodes:]
        right_ref[inner:, at] = jnp.where(is_last, paired, jnp.zeros_like(paired))
    for s in range(blocks):
        part = dot(rows_ref[s, :inner], right_ref[:inner], ((0,), (0,)))
        part += dot(rows_ref[s, nodes:], right_ref[inner:], ((0,), (0,)))
        scatter_rows(part, out_ref, s)


def gram_other_kernel(rows_ref, right_ref, out_ref):
    blocks, total, _ = rows_ref.shape
    nodes = right_ref.shape[0]
    inner = 2 * nodes - total
    for s in range(blocks):
        part = dot(rows_ref[s, :inner], right_ref[:inner], ((0,), (0,)))
        part += dot(rows_ref[s, nodes:], right_ref[inner:], ((0,), (0,)))
        scatter_rows(part, out_ref, s)


def gram_shapes(blocks, orb):
    xs, ys = lax.axis_size("x"), lax.axis_size("y")
    return jax.ShapeDtypeStruct((xs, ys, blocks, orb // xs, 2 * blocks * orb // ys), bf16)


def gram_own(where, matrices, rows):
    blocks, total, orb = rows.shape
    nodes = matrices.shape[1]
    out = gram_shapes(blocks, orb)
    return pl.pallas_call(
        gram_own_kernel,
        grid_spec=pltpu.PrefetchScalarGridSpec(
            num_scalar_prefetch=1,
            grid=(1,),
            in_specs=[
                pl.BlockSpec((1, nodes, nodes), lambda i, w: (w[0], 0, 0)),
                pl.BlockSpec(rows.shape, lambda i, w: (0, 0, 0)),
            ],
            out_specs=[
                pl.BlockSpec(out.shape, lambda i, w: (0,) * 5),
                pl.BlockSpec((nodes, 2 * blocks * orb), lambda i, w: (0, 0)),
            ],
        ),
        out_shape=[out, jax.ShapeDtypeStruct((nodes, 2 * blocks * orb), bf16)],
        name="gram_own",
    )(where, matrices, rows)


def gram_other(rows, right):
    return pl.pallas_call(
        gram_other_kernel,
        out_shape=gram_shapes(rows.shape[0], rows.shape[2]),
        name="gram_other",
    )(rows, right)


def summed(parts):
    return jnp.sum(parts.astype(f32), 0).astype(bf16)


def swap_sum(part, axis):
    return summed(lax.all_to_all(part, axis, split_axis=0, concat_axis=0, tiled=True))


def local(cell_matrices, initial_states, face_map):
    face = face_map.shape[1]
    cells_dev, nodes = cell_matrices.shape[:2]
    orb_dev = initial_states.shape[2]
    elems = lax.axis_size(elem)
    zhs, cores, zls = lax.axis_size("zh"), lax.axis_size("core"), lax.axis_size("zl")
    xs, ys = lax.axis_size("x"), lax.axis_size("y")
    onehot = (face_map[:, :, None] == jnp.arange(face, dtype=jnp.int32)[None, None, :]).astype(bf16)
    matrices = reordered(cell_matrices, onehot)

    def to_next_order(faces):
        return jnp.einsum("cfm,cfo->cmo", onehot, faces, preferred_element_type=f32)

    def edges(values):
        return (
            dot(matrices[0, :face], values[0]),
            dot(matrices[-1, -face:], values[-1]),
        )

    start_upper = to_next_order(initial_states[:, -face:])
    current_b = jnp.concatenate([initial_states[:, :-face], start_upper.astype(bf16)], 1)
    start = current_b.astype(f32)
    previous = start
    current = start
    next_start = None
    for degree in range(PASSES):
        head, tail = edges(current_b)
        if degree == 0:
            both = shifted(jnp.stack([head, start[0, :face]]), False)
            from_above, next_start = both[0], both[1]
        else:
            from_above = shifted(head, False)
        from_below = shifted(tail, True)
        products = jnp.einsum("cij,cjo->cio", matrices, current_b, preferred_element_type=f32)
        from_next = jnp.concatenate([products[1:, :face], from_above[None]], 0)
        from_low = jnp.concatenate([from_below[None], products[:-1, -face:]], 0)
        image = jnp.concatenate(
            [
                products[:, :face] + from_low,
                products[:, face:-face],
                products[:, -face:] + from_next,
            ],
            1,
        )
        following = image / filter_width if degree == 0 else 2.0 / filter_width * image - previous
        previous = current
        current = following
        current_b = following.astype(bf16)

    place = lax.axis_index(elem) * cells_dev
    cell_index = place + jnp.arange(cells_dev, dtype=jnp.int32)
    is_last = cell_index == cells_dev * elems - 1
    step = start[:, -face:] - jnp.concatenate([start[1:, :face], next_start[None]], 0)
    step = jnp.where(is_last[:, None, None], 0.0, step)
    paired = (current[:, -face:] - step).astype(bf16)

    rows = jnp.concatenate([current_b, paired], 1)
    rows = lax.all_to_all(rows, "zh", split_axis=0, concat_axis=0, tiled=True)
    other = lax.ppermute(rows, "core", [(0, 1), (1, 0)])
    zh = lax.axis_index("zh")
    where = jnp.stack([zh, (place + zh == cells_dev * elems - 1).astype(jnp.int32)])
    own_part, right = gram_own(where, matrices, rows)
    other_part = gram_other(other, right)
    own_part = swap_sum(swap_sum(own_part, "x"), "y")
    other_part = swap_sum(swap_sum(other_part, "x"), "y")
    is_first = lax.axis_index("core") == 0
    by_core = jnp.stack(
        [jnp.where(is_first, own_part, other_part), jnp.where(is_first, other_part, own_part)], 1
    )
    sub, cols = by_core.shape[2:]
    column = jnp.broadcast_to(by_core[None], (zls,) + by_core.shape).reshape(-1, sub, cols)
    column = lax.all_to_all(column, ("zl", "zh", "core"), split_axis=0, concat_axis=0, tiled=True)
    piece = summed(column.reshape(zls * zhs, cores, sub, cols))
    whole = lax.all_gather(piece, ("y", "x"), axis=0, tiled=False)
    whole = whole.reshape(ys, xs, cores, sub, cols).transpose(1, 3, 2, 0, 4)
    whole = whole.reshape(xs, sub, cores, 2, zhs, orb_dev).transpose(3, 0, 1, 4, 2, 5)
    whole = whole.reshape(2, orb_dev, zhs * cores * orb_dev)
    whole = whole.astype(f32) * (1.0 / (cells_dev * elems * nodes))

    upper = jnp.einsum("cfm,cmo->cfo", onehot, current_b[:, -face:], preferred_element_type=f32)
    states = jnp.concatenate([current_b[:, :-face], upper.astype(bf16)], 1)
    return (states, whole[0], whole[1])


def solution(mesh):
    names = elem + state
    fine = Mesh(mesh.devices.reshape([size for _, size in ELEM + STATE]), names)
    return jax.shard_map(
        local,
        mesh=fine,
        in_specs=(P(elem, None, None), P(elem, None, state), P(elem, None)),
        out_specs=(P(elem, None, state), P(state, None), P(state, None)),
        check_vma=False,
    )
```

```python
import jax
import jax.numpy as jnp
from jax import lax
from jax.experimental import pallas as pl
from jax.experimental.pallas import tpu as pltpu
from jax.sharding import Mesh
from jax.sharding import PartitionSpec as P

PASSES = 4
ELEM = (("y", 8), ("x", 4), ("zl", 3))
STATE = (("zh", 4), ("core", 2))


filter_width = 2.5

f32 = jnp.float32
bf16 = jnp.bfloat16
elem = tuple(name for name, _ in ELEM)
state = tuple(name for name, _ in STATE)


def dot(a, b, dims=((1,), (0,))):
    return lax.dot_general(a, b, (dims, ((), ())), preferred_element_type=f32)


def shifted(faces, up):
    count = lax.axis_size(elem)
    pairs = [(i, i + 1) if up else (i + 1, i) for i in range(count - 1)]
    return lax.ppermute(faces, elem, pairs)


def vmem():
    return pl.BlockSpec(memory_space=pltpu.VMEM)


def smem():
    return pl.BlockSpec(memory_space=pltpu.SMEM)


SMALL = pltpu.CompilerParams(vmem_limit_bytes=20 * 1024 * 1024)


def selection(map_row):
    face = map_row.shape[1]
    rows = lax.broadcasted_iota(jnp.int32, (face, face), 0)
    return jnp.where(rows == map_row, 1.0, 0.0).astype(bf16)


def first_edges_kernel(map_ref, low_ref, up_ref, first_ref, last_ref, head_ref, tail_ref):
    face = low_ref.shape[1]
    head_ref[0] = dot(low_ref[0], first_ref[0])
    head_ref[1] = first_ref[0, :face].astype(f32)
    cells = map_ref.shape[0]
    up = dot(selection(map_ref[cells - 1 :, :]), up_ref[0]).astype(bf16)
    tail_ref[...] = dot(up, last_ref[0])


def first_edges(cell_matrices, states, face_map):
    cells, nodes, orb = states.shape
    face = face_map.shape[1]
    return pl.pallas_call(
        first_edges_kernel,
        grid=(1,),
        in_specs=[
            pl.BlockSpec((cells, face), lambda i: (0, 0)),
            pl.BlockSpec((1, face, nodes), lambda i: (0, 0, 0)),
            pl.BlockSpec((1, face, nodes), lambda i: (cells - 1, nodes // face - 1, 0)),
            pl.BlockSpec((1, nodes, orb), lambda i: (0, 0, 0)),
            pl.BlockSpec((1, nodes, orb), lambda i: (cells - 1, 0, 0)),
        ],
        out_specs=[
            pl.BlockSpec((2, face, orb), lambda i: (0, 0, 0)),
            pl.BlockSpec((face, orb), lambda i: (0, 0)),
        ],
        out_shape=[
            jax.ShapeDtypeStruct((2, face, orb), f32),
            jax.ShapeDtypeStruct((face, orb), f32),
        ],
        compiler_params=SMALL,
        name="first_edges",
    )(face_map, cell_matrices, cell_matrices, states, states)


def reorder_kernel(map_ref, k_ref, x_ref, out_ref, start_ref):
    face = map_ref.shape[2]
    nodes = k_ref.shape[1]
    inner = nodes - face
    select = selection(map_ref[0])
    wide = 2 * face
    eye = lax.broadcasted_iota(jnp.int32, (wide, wide), 0) == lax.broadcasted_iota(jnp.int32, (wide, wide), 1)
    both = jnp.concatenate([jnp.zeros((face, face), bf16), select], 1)
    both = jnp.concatenate([jnp.where(eye[:face], 1.0, 0.0).astype(bf16), both], 0)
    out_ref[0, :, : nodes - wide] = k_ref[0, :, : nodes - wide]
    out_ref[0, :, nodes - wide :] = dot(k_ref[0, :, nodes - wide :], both, ((1,), (1,))).astype(bf16)
    out_ref[0, inner:, :] = dot(select, out_ref[0, inner:, :]).astype(bf16)
    start_ref[0, :inner] = x_ref[0, :inner]
    start_ref[0, inner:] = dot(select, x_ref[0, inner:]).astype(bf16)


def reordered(cell_matrices, states, face_map):
    cells, nodes = cell_matrices.shape[:2]
    orb = states.shape[2]
    face = face_map.shape[1]
    per_cell = lambda *shape: pl.BlockSpec((1,) + shape, lambda c: (c, 0, 0))
    return pl.pallas_call(
        reorder_kernel,
        grid=(cells,),
        in_specs=[per_cell(1, face), per_cell(nodes, nodes), per_cell(nodes, orb)],
        out_specs=[per_cell(nodes, nodes), per_cell(nodes, orb)],
        out_shape=[
            jax.ShapeDtypeStruct(cell_matrices.shape, bf16),
            jax.ShapeDtypeStruct(states.shape, bf16),
        ],
        compiler_params=SMALL,
        name="reorder",
    )(face_map[:, None, :], cell_matrices, states)


def scatter_rows(part, out_ref, block, core):
    xs, ys, _, _, rows, cols = out_ref.shape
    for x in range(xs):
        for y in range(ys):
            tile = part[x * rows : (x + 1) * rows, y * cols : (y + 1) * cols].astype(bf16)
            out_ref[x, y, block, core] = tile


def right_kernel(where_ref, k_ref, rows_ref, right_ref):
    blocks, total, orb = rows_ref.shape
    nodes = k_ref.shape[1]
    inner = 2 * nodes - total
    is_last = where_ref[1] == 1
    matrix = k_ref[where_ref[0]]
    for s in range(blocks):
        at = slice(s * orb, (s + 1) * orb)
        right_ref[:, at] = dot(matrix, rows_ref[s, :nodes]).astype(bf16)
        at = slice((blocks + s) * orb, (blocks + s + 1) * orb)
        right_ref[:inner, at] = rows_ref[s, :inner]
        paired = rows_ref[s, nodes:]
        right_ref[inner:, at] = jnp.where(is_last, paired, jnp.zeros_like(paired))


def gram_kernel(where_ref, own_ref, other_ref, right_ref, out_ref, left_ref):
    blocks, total, _ = own_ref.shape
    nodes = right_ref.shape[0]
    inner = 2 * nodes - total
    for ref, core in ((own_ref, where_ref[2]), (other_ref, 1 - where_ref[2])):
        for s in range(blocks):
            left_ref[:inner] = ref[s, :inner]
            left_ref[inner:] = ref[s, nodes:]
            part = dot(left_ref[...], right_ref[...], ((0,), (0,)))
            scatter_rows(part, out_ref, s, core)


def right_of(where, matrices, rows):
    blocks, _, orb = rows.shape
    nodes = matrices.shape[1]
    return pl.pallas_call(
        right_kernel,
        in_specs=[smem(), vmem(), vmem()],
        out_specs=vmem(),
        out_shape=jax.ShapeDtypeStruct((nodes, 2 * blocks * orb), bf16),
        compiler_params=SMALL,
        name="right",
    )(where, matrices, rows)


def gram(where, own, other, right):
    blocks, _, orb = own.shape
    xs, ys, cores = lax.axis_size("x"), lax.axis_size("y"), lax.axis_size("core")
    shape = (xs, ys, blocks, cores, orb // xs, 2 * blocks * orb // ys)
    return pl.pallas_call(
        gram_kernel,
        in_specs=[smem(), vmem(), vmem(), vmem()],
        out_specs=vmem(),
        out_shape=jax.ShapeDtypeStruct(shape, bf16),
        scratch_shapes=[pltpu.VMEM((right.shape[0], orb), bf16)],
        compiler_params=SMALL,
        name="gram",
    )(where, own, other, right)


def assemble_kernel(scale, pieces_ref, ham_ref, inter_ref):
    ys, xs, cores, sub, cols = pieces_ref.shape
    orb = sub * xs
    for out_ref, half in ((ham_ref, 0), (inter_ref, 1)):
        for y in range(ys // 2):
            for k in range(cols // orb):
                zh = y * cols // orb + k
                for c in range(cores):
                    for x in range(xs):
                        tile = pieces_ref[half * ys // 2 + y, x, c, :, k * orb : (k + 1) * orb]
                        at = (zh * cores + c) * orb
                        out_ref[x * sub : (x + 1) * sub, at : at + orb] = tile.astype(f32) * scale


def assemble(pieces, scale):
    ys, xs, cores, sub, cols = pieces.shape
    out = jax.ShapeDtypeStruct((sub * xs, ys * cores * cols // 2), f32)
    return pl.pallas_call(
        lambda *refs: assemble_kernel(scale, *refs),
        in_specs=[vmem()],
        out_specs=[vmem(), vmem()],
        out_shape=[out, out],
        compiler_params=SMALL,
        name="assemble",
    )(pieces)


def summed(parts):
    return jnp.sum(parts.astype(f32), 0).astype(bf16)


def swap_sum(part, axis):
    return summed(lax.all_to_all(part, axis, split_axis=0, concat_axis=0, tiled=True))


def local(cell_matrices, initial_states, face_map):
    face = face_map.shape[1]
    cells_dev, nodes = cell_matrices.shape[:2]
    orb_dev = initial_states.shape[2]
    elems = lax.axis_size(elem)
    zhs, cores, zls = lax.axis_size("zh"), lax.axis_size("core"), lax.axis_size("zl")
    xs, ys = lax.axis_size("x"), lax.axis_size("y")
    head, tail = first_edges(cell_matrices, initial_states, face_map)
    cell_matrices, initial_states, head, tail = lax.optimization_barrier(
        (cell_matrices, initial_states, head, tail)
    )
    both = shifted(head, False)
    from_below = shifted(tail, True)
    matrices, current_b = reordered(cell_matrices, initial_states, face_map)

    def edges(values):
        return (
            dot(matrices[0, :face], values[0]),
            dot(matrices[-1, -face:], values[-1]),
        )

    start = current_b.astype(f32)
    previous = start
    current = start
    from_above, next_start = both[0], both[1]
    for degree in range(PASSES):
        if degree > 0:
            head, tail = edges(current_b)
            from_above = shifted(head, False)
            from_below = shifted(tail, True)
        products = jnp.einsum("cij,cjo->cio", matrices, current_b, preferred_element_type=f32)
        from_next = jnp.concatenate([products[1:, :face], from_above[None]], 0)
        from_low = jnp.concatenate([from_below[None], products[:-1, -face:]], 0)
        image = jnp.concatenate(
            [
                products[:, :face] + from_low,
                products[:, face:-face],
                products[:, -face:] + from_next,
            ],
            1,
        )
        following = image / filter_width if degree == 0 else 2.0 / filter_width * image - previous
        previous = current
        current = following
        current_b = following.astype(bf16)

    place = lax.axis_index(elem) * cells_dev
    cell_index = place + jnp.arange(cells_dev, dtype=jnp.int32)
    is_last = cell_index == cells_dev * elems - 1
    step = start[:, -face:] - jnp.concatenate([start[1:, :face], next_start[None]], 0)
    step = jnp.where(is_last[:, None, None], 0.0, step)
    paired = (current[:, -face:] - step).astype(bf16)

    rows = jnp.concatenate([current_b, paired], 1)
    rows = lax.all_to_all(rows, "zh", split_axis=0, concat_axis=0, tiled=True)
    other = lax.ppermute(rows, "core", [(0, 1), (1, 0)])
    zh = lax.axis_index("zh")
    at_end = (place + zh == cells_dev * elems - 1).astype(jnp.int32)
    where = jnp.stack([zh, at_end, lax.axis_index("core")])
    right = right_of(where, matrices, rows)
    part = gram(where, rows, other, right)
    part = swap_sum(part, "x")
    part = swap_sum(part, "y")
    sub, cols = part.shape[2:]
    column = jnp.broadcast_to(part[None], (zls,) + part.shape).reshape(-1, sub, cols)
    column = lax.all_to_all(column, ("zl", "zh", "core"), split_axis=0, concat_axis=0, tiled=True)
    piece = summed(column.reshape(zls * zhs, cores, sub, cols))
    pieces = jnp.broadcast_to(piece[None], (ys * xs,) + piece.shape)
    pieces = lax.all_to_all(pieces, ("y", "x"), split_axis=0, concat_axis=0, tiled=True)
    scale = 1.0 / (cells_dev * elems * nodes)
    hamiltonian, intersection = assemble(pieces.reshape(ys, xs, cores, sub, cols), scale)

    onehot = (face_map[:, :, None] == jnp.arange(face, dtype=jnp.int32)[None, None, :]).astype(bf16)
    upper = jnp.einsum("cfm,cmo->cfo", onehot, current_b[:, -face:], preferred_element_type=f32)
    states = jnp.concatenate([current_b[:, :-face], upper.astype(bf16)], 1)
    return (states, hamiltonian, intersection)


def solution(mesh):
    names = elem + state
    fine = Mesh(mesh.devices.reshape([size for _, size in ELEM + STATE]), names)
    return jax.shard_map(
        local,
        mesh=fine,
        in_specs=(P(elem, None, None), P(elem, None, state), P(elem, None)),
        out_specs=(P(elem, None, state), P(state, None), P(state, None)),
        check_vma=False,
    )
```

```python
import jax
import jax.numpy as jnp
from jax import lax
from jax.experimental import pallas as pl
from jax.experimental.pallas import tpu as pltpu
from jax.sharding import Mesh
from jax.sharding import PartitionSpec as P

PASSES = 4
ELEM = (("y", 8), ("x", 4), ("zl", 3))
STATE = (("zh", 4), ("core", 2))


filter_width = 2.5

f32 = jnp.float32
bf16 = jnp.bfloat16
elem = tuple(name for name, _ in ELEM)
state = tuple(name for name, _ in STATE)


def dot(a, b, dims=((1,), (0,))):
    return lax.dot_general(a, b, (dims, ((), ())), preferred_element_type=f32)


def shifted(faces, up):
    count = lax.axis_size(elem)
    pairs = [(i, i + 1) if up else (i + 1, i) for i in range(count - 1)]
    return lax.ppermute(faces, elem, pairs)


def vmem():
    return pl.BlockSpec(memory_space=pltpu.VMEM)


def smem():
    return pl.BlockSpec(memory_space=pltpu.SMEM)


SMALL = pltpu.CompilerParams(vmem_limit_bytes=20 * 1024 * 1024)


def selection(map_row):
    face = map_row.shape[1]
    rows = lax.broadcasted_iota(jnp.int32, (face, face), 0)
    return jnp.where(rows == map_row, 1.0, 0.0).astype(bf16)


def first_edges_kernel(map_ref, low_ref, up_ref, first_ref, last_ref, head_ref, tail_ref):
    face = low_ref.shape[1]
    head_ref[0] = dot(low_ref[0], first_ref[0])
    head_ref[1] = first_ref[0, :face].astype(f32)
    cells = map_ref.shape[0]
    up = dot(selection(map_ref[cells - 1 :, :]), up_ref[0]).astype(bf16)
    tail_ref[...] = dot(up, last_ref[0])


def first_edges(cell_matrices, states, face_map):
    cells, nodes, orb = states.shape
    face = face_map.shape[1]
    return pl.pallas_call(
        first_edges_kernel,
        grid=(1,),
        in_specs=[
            pl.BlockSpec((cells, face), lambda i: (0, 0)),
            pl.BlockSpec((1, face, nodes), lambda i: (0, 0, 0)),
            pl.BlockSpec((1, face, nodes), lambda i: (cells - 1, nodes // face - 1, 0)),
            pl.BlockSpec((1, nodes, orb), lambda i: (0, 0, 0)),
            pl.BlockSpec((1, nodes, orb), lambda i: (cells - 1, 0, 0)),
        ],
        out_specs=[
            pl.BlockSpec((2, face, orb), lambda i: (0, 0, 0)),
            pl.BlockSpec((face, orb), lambda i: (0, 0)),
        ],
        out_shape=[
            jax.ShapeDtypeStruct((2, face, orb), f32),
            jax.ShapeDtypeStruct((face, orb), f32),
        ],
        compiler_params=SMALL,
        name="first_edges",
    )(face_map, cell_matrices, cell_matrices, states, states)


def reorder_kernel(map_ref, k_ref, x_ref, out_ref, start_ref, wide_ref, product_ref):
    cells, nodes, _ = k_ref.shape
    face = map_ref.shape[1]
    inner = nodes - face
    wide = 2 * face
    eye = lax.broadcasted_iota(jnp.int32, (wide, wide), 0) == lax.broadcasted_iota(jnp.int32, (wide, wide), 1)
    eye = jnp.where(eye[:face], 1.0, 0.0).astype(bf16)
    for c in range(cells):
        select = selection(map_ref[c : c + 1, :])
        both = jnp.concatenate([jnp.zeros((face, face), bf16), select], 1)
        both = jnp.concatenate([eye, both], 0)
        out_ref[c, :, : nodes - wide] = k_ref[c, :, : nodes - wide]
        out_ref[c, :, nodes - wide :] = dot(k_ref[c, :, nodes - wide :], both, ((1,), (1,))).astype(bf16)
        out_ref[c, inner:, :] = dot(select, out_ref[c, inner:, :]).astype(bf16)
        start_ref[c, :inner] = x_ref[c, :inner]
        start_ref[c, inner:] = dot(select, x_ref[c, inner:]).astype(bf16)
        wide_ref[c] = start_ref[c].astype(f32)
        product_ref[c] = dot(out_ref[c], start_ref[c])


def reordered(cell_matrices, states, face_map):
    return pl.pallas_call(
        reorder_kernel,
        in_specs=[vmem()] * 3,
        out_specs=[vmem()] * 4,
        out_shape=[
            jax.ShapeDtypeStruct(cell_matrices.shape, bf16),
            jax.ShapeDtypeStruct(states.shape, bf16),
            jax.ShapeDtypeStruct(states.shape, f32),
            jax.ShapeDtypeStruct(states.shape, f32),
        ],
        compiler_params=SMALL,
        name="reorder",
    )(face_map, cell_matrices, states)


def scatter_rows(part, out_ref, block, core, place):
    half = out_ref.shape[1]
    rows, cols = out_ref.shape[-2:]
    for x in range(part.shape[0] // rows):
        away = lax.rem(x - place + 4, 4)
        slots = (
            jnp.where(away == 0, 4, jnp.where(away == 1, 6, jnp.where(away == 2, 0, 3))),
            jnp.where(away == 0, 5, jnp.where(away == 1, 1, jnp.where(away == 2, 2, 7))),
        )
        for y in range(2 * half):
            tile = part[x * rows : (x + 1) * rows, y * cols : (y + 1) * cols].astype(bf16)
            out_ref[slots[y // half], y % half, block, core] = tile


def pack_kernel(where_ref, now_ref, start_ref, next_ref, own_ref, up_ref, down_ref):
    cells, nodes, _ = now_ref.shape
    face = next_ref.shape[0]
    total = nodes + face
    inner = nodes - face
    half = total // 2
    last_cell = where_ref[3]

    def rows_of(away):
        c = lax.rem(where_ref[0] + away, cells)
        now = now_ref[c]
        after = jnp.where(c == cells - 1, next_ref[...], start_ref[lax.rem(c + 1, cells), :face])
        step = jnp.where(c == last_cell, 0.0, start_ref[c, inner:] - after)
        paired = (now[inner:] - step).astype(bf16)
        return now.astype(bf16), paired

    for away, ref in ((0, own_ref), (1, up_ref), (3, down_ref)):
        now, paired = rows_of(away)
        ref[:nodes] = now
        ref[nodes:total] = paired
    now, paired = rows_of(2)
    up_ref[total:] = now[:half]
    down_ref[total : total + nodes - half] = now[half:]
    down_ref[total + nodes - half :] = paired


def pack(where, now, start, after):
    cells, nodes, orb = now.shape
    total = nodes + after.shape[0]
    sent = jax.ShapeDtypeStruct((total + total // 2, orb), bf16)
    return pl.pallas_call(
        pack_kernel,
        in_specs=[smem()] + [vmem()] * 3,
        out_specs=[vmem()] * 3,
        out_shape=[jax.ShapeDtypeStruct((total, orb), bf16), sent, sent],
        compiler_params=SMALL,
        name="pack",
    )(where, now, start, after)


def collect_kernel(where_ref, own_ref, below_ref, above_ref, low_half_ref, high_half_ref, rows_ref):
    cells, total, _ = rows_ref.shape
    half = total // 2
    place = where_ref[0]
    rows_ref[place] = own_ref[...]
    rows_ref[lax.rem(place + 3, cells)] = below_ref[:total]
    rows_ref[lax.rem(place + 1, cells)] = above_ref[:total]
    far = lax.rem(place + 2, cells)
    rows_ref[far, :half] = low_half_ref[...]
    rows_ref[far, half:] = high_half_ref[...]


def collect(where, own, below, above, low_half, high_half):
    total, orb = own.shape
    return pl.pallas_call(
        collect_kernel,
        in_specs=[smem()] + [vmem()] * 5,
        out_specs=vmem(),
        out_shape=jax.ShapeDtypeStruct((4, total, orb), bf16),
        compiler_params=SMALL,
        name="collect",
    )(where, own, below, above, low_half, high_half)


def right_kernel(where_ref, k_ref, rows_ref, right_ref):
    blocks, total, orb = rows_ref.shape
    nodes = k_ref.shape[1]
    inner = 2 * nodes - total
    is_last = where_ref[1] == 1
    matrix = k_ref[where_ref[0]]
    for s in range(blocks):
        at = slice(s * orb, (s + 1) * orb)
        right_ref[:, at] = dot(matrix, rows_ref[s, :nodes]).astype(bf16)
        at = slice((blocks + s) * orb, (blocks + s + 1) * orb)
        right_ref[:inner, at] = rows_ref[s, :inner]
        paired = rows_ref[s, nodes:]
        right_ref[inner:, at] = jnp.where(is_last, paired, jnp.zeros_like(paired))


def gram_kernel(where_ref, own_ref, other_ref, right_ref, out_ref, left_ref):
    blocks, total, _ = own_ref.shape
    nodes = right_ref.shape[0]
    inner = 2 * nodes - total
    for ref, core in ((own_ref, where_ref[2]), (other_ref, 1 - where_ref[2])):
        for s in range(blocks):
            left_ref[:inner] = ref[s, :inner]
            left_ref[inner:] = ref[s, nodes:]
            part = dot(left_ref[...], right_ref[...], ((0,), (0,)))
            scatter_rows(part, out_ref, s, core, where_ref[4])


def right_of(where, matrices, rows):
    blocks, _, orb = rows.shape
    nodes = matrices.shape[1]
    return pl.pallas_call(
        right_kernel,
        in_specs=[smem(), vmem(), vmem()],
        out_specs=vmem(),
        out_shape=jax.ShapeDtypeStruct((nodes, 2 * blocks * orb), bf16),
        compiler_params=SMALL,
        name="right",
    )(where, matrices, rows)


def gram(where, own, other, right):
    blocks, _, orb = own.shape
    xs, ys, cores = lax.axis_size("x"), lax.axis_size("y"), lax.axis_size("core")
    shape = (2 * xs, ys // 2, blocks, cores, orb // xs, 2 * blocks * orb // ys)
    return pl.pallas_call(
        gram_kernel,
        in_specs=[smem(), vmem(), vmem(), vmem()],
        out_specs=vmem(),
        out_shape=jax.ShapeDtypeStruct(shape, bf16),
        scratch_shapes=[pltpu.VMEM((right.shape[0], orb), bf16)],
        compiler_params=SMALL,
        name="gram",
    )(where, own, other, right)


def assemble_kernel(scale, pieces_ref, ham_ref, inter_ref):
    ys, xs, cores, sub, cols = pieces_ref.shape
    orb = sub * xs
    for out_ref, half in ((ham_ref, 0), (inter_ref, 1)):
        for y in range(ys // 2):
            for k in range(cols // orb):
                zh = y * cols // orb + k
                for c in range(cores):
                    for x in range(xs):
                        tile = pieces_ref[half * ys // 2 + y, x, c, :, k * orb : (k + 1) * orb]
                        at = (zh * cores + c) * orb
                        out_ref[x * sub : (x + 1) * sub, at : at + orb] = tile.astype(f32) * scale


def assemble(pieces, scale):
    ys, xs, cores, sub, cols = pieces.shape
    out = jax.ShapeDtypeStruct((sub * xs, ys * cores * cols // 2), f32)
    return pl.pallas_call(
        lambda *refs: assemble_kernel(scale, *refs),
        in_specs=[vmem()],
        out_specs=[vmem(), vmem()],
        out_shape=[out, out],
        compiler_params=SMALL,
        name="assemble",
    )(pieces)


def summed(parts):
    return jnp.sum(parts.astype(f32), 0).astype(bf16)


def ring(part, axis, step):
    count = lax.axis_size(axis)
    return lax.ppermute(part, axis, [(i, (i + step) % count) for i in range(count)])


def added(*parts):
    return sum(part.astype(f32) for part in parts).astype(bf16)


def x_sum(part):
    below = ring(part[0:2], "x", 1)
    above = ring(part[2:4], "x", -1)
    below_2 = ring(added(below[0], part[6]), "x", 1)
    above_2 = ring(added(above[0], part[7]), "x", -1)
    return jnp.concatenate([added(part[4], above[1], below_2), added(part[5], below[1], above_2)], 0)


def swap_sum(part, axis):
    return summed(lax.all_to_all(part, axis, split_axis=0, concat_axis=0, tiled=True))


def local(cell_matrices, initial_states, face_map):
    face = face_map.shape[1]
    cells_dev, nodes = cell_matrices.shape[:2]
    orb_dev = initial_states.shape[2]
    elems = lax.axis_size(elem)
    zhs, cores, zls = lax.axis_size("zh"), lax.axis_size("core"), lax.axis_size("zl")
    xs, ys = lax.axis_size("x"), lax.axis_size("y")
    head, tail = first_edges(cell_matrices, initial_states, face_map)
    cell_matrices, initial_states, head, tail = lax.optimization_barrier(
        (cell_matrices, initial_states, head, tail)
    )
    both = shifted(head, False)
    from_below = shifted(tail, True)
    matrices, current_b, start, products = reordered(cell_matrices, initial_states, face_map)

    def edges(values):
        return (
            dot(matrices[0, :face], values[0]),
            dot(matrices[-1, -face:], values[-1]),
        )

    previous = start
    current = start
    from_above, next_start = both[0], both[1]
    for degree in range(PASSES):
        if degree > 0:
            head, tail = edges(current_b)
            from_above = shifted(head, False)
            from_below = shifted(tail, True)
            current_b, head, tail = lax.optimization_barrier((current_b, head, tail))
            products = jnp.einsum("cij,cjo->cio", matrices, current_b, preferred_element_type=f32)
        from_next = jnp.concatenate([products[1:, :face], from_above[None]], 0)
        from_low = jnp.concatenate([from_below[None], products[:-1, -face:]], 0)
        image = jnp.concatenate(
            [
                products[:, :face] + from_low,
                products[:, face:-face],
                products[:, -face:] + from_next,
            ],
            1,
        )
        following = image / filter_width if degree == 0 else 2.0 / filter_width * image - previous
        previous = current
        current = following
        current_b = following.astype(bf16)

    place = lax.axis_index(elem) * cells_dev
    zh = lax.axis_index("zh")
    last_cell = cells_dev * elems - 1 - place
    where = jnp.stack(
        [zh, (zh == last_cell).astype(jnp.int32), lax.axis_index("core"), last_cell, lax.axis_index("x")]
    )

    own, up, down = pack(where, current, start, next_start)
    total = own.shape[0]
    below = ring(up, "zh", 1)
    above = ring(down, "zh", -1)
    low_half = ring(below[total:], "zh", 1)
    high_half = ring(above[total:], "zh", -1)
    rows = collect(where, own, below, above, low_half, high_half)
    other = ring(rows, "core", 1)
    right = right_of(where, matrices, rows)
    part = gram(where, rows, other, right)
    part = x_sum(part)
    part = swap_sum(part, "y")
    sub, cols = part.shape[2:]
    column = jnp.broadcast_to(part[None], (zls,) + part.shape).reshape(-1, sub, cols)
    column = lax.all_to_all(column, ("zl", "zh", "core"), split_axis=0, concat_axis=0, tiled=True)
    piece = summed(column.reshape(zls * zhs, cores, sub, cols))
    pieces = jnp.broadcast_to(piece[None], (ys * xs,) + piece.shape)
    pieces = lax.all_to_all(pieces, ("y", "x"), split_axis=0, concat_axis=0, tiled=True)
    scale = 1.0 / (cells_dev * elems * nodes)
    hamiltonian, intersection = assemble(pieces.reshape(ys, xs, cores, sub, cols), scale)

    onehot = (face_map[:, :, None] == jnp.arange(face, dtype=jnp.int32)[None, None, :]).astype(bf16)
    upper = jnp.einsum("cfm,cmo->cfo", onehot, current_b[:, -face:], preferred_element_type=f32)
    states = jnp.concatenate([current_b[:, :-face], upper.astype(bf16)], 1)
    return (states, hamiltonian, intersection)


def solution(mesh):
    names = elem + state
    fine = Mesh(mesh.devices.reshape([size for _, size in ELEM + STATE]), names)
    return jax.shard_map(
        local,
        mesh=fine,
        in_specs=(P(elem, None, None), P(elem, None, state), P(elem, None)),
        out_specs=(P(elem, None, state), P(state, None), P(state, None)),
        check_vma=False,
    )
```

```python
import jax
import jax.numpy as jnp
from jax import lax
from jax.experimental import pallas as pl
from jax.experimental.pallas import tpu as pltpu
from jax.sharding import Mesh
from jax.sharding import PartitionSpec as P

PASSES = 4
ELEM = (("y", 8), ("x", 4), ("zl", 3))
STATE = (("zh", 4), ("core", 2))


filter_width = 2.5

f32 = jnp.float32
bf16 = jnp.bfloat16
elem = tuple(name for name, _ in ELEM)
state = tuple(name for name, _ in STATE)


def dot(a, b, dims=((1,), (0,))):
    return lax.dot_general(a, b, (dims, ((), ())), preferred_element_type=f32)


def neighbours(head, tail):
    count = lax.axis_size(elem)
    even = lax.axis_index(elem) % 2 == 0
    swaps = []
    for first, sent in ((1, jnp.where(even, head, tail)), (0, jnp.where(even, tail, head))):
        pairs = [(i, i + 1) for i in range(first, count - 1, 2)]
        swaps.append(lax.ppermute(sent, elem, pairs + [(j, i) for i, j in pairs]))
    return jnp.where(even, swaps[1], swaps[0]), jnp.where(even, swaps[0], swaps[1])


def vmem():
    return pl.BlockSpec(memory_space=pltpu.VMEM)


def smem():
    return pl.BlockSpec(memory_space=pltpu.SMEM)


SMALL = pltpu.CompilerParams(vmem_limit_bytes=20 * 1024 * 1024)


def selection(map_row):
    face = map_row.shape[1]
    rows = lax.broadcasted_iota(jnp.int32, (face, face), 0)
    return jnp.where(rows == map_row, 1.0, 0.0).astype(bf16)


def first_edges_kernel(map_ref, low_ref, up_ref, first_ref, last_ref, head_ref, tail_ref):
    face = low_ref.shape[1]
    head_ref[0] = dot(low_ref[0], first_ref[0])
    head_ref[1] = first_ref[0, :face].astype(f32)
    cells = map_ref.shape[0]
    up = dot(selection(map_ref[cells - 1 :, :]), up_ref[0]).astype(bf16)
    tail_ref[0] = dot(up, last_ref[0])
    tail_ref[1] = jnp.zeros_like(tail_ref[1])


def first_edges(cell_matrices, states, face_map):
    cells, nodes, orb = states.shape
    face = face_map.shape[1]
    return pl.pallas_call(
        first_edges_kernel,
        grid=(1,),
        in_specs=[
            pl.BlockSpec((cells, face), lambda i: (0, 0)),
            pl.BlockSpec((1, face, nodes), lambda i: (0, 0, 0)),
            pl.BlockSpec((1, face, nodes), lambda i: (cells - 1, nodes // face - 1, 0)),
            pl.BlockSpec((1, nodes, orb), lambda i: (0, 0, 0)),
            pl.BlockSpec((1, nodes, orb), lambda i: (cells - 1, 0, 0)),
        ],
        out_specs=[
            pl.BlockSpec((2, face, orb), lambda i: (0, 0, 0)),
            pl.BlockSpec((2, face, orb), lambda i: (0, 0, 0)),
        ],
        out_shape=[
            jax.ShapeDtypeStruct((2, face, orb), f32),
            jax.ShapeDtypeStruct((2, face, orb), f32),
        ],
        compiler_params=SMALL,
        name="first_edges",
    )(face_map, cell_matrices, cell_matrices, states, states)


def reorder_kernel(map_ref, k_ref, x_ref, out_ref, start_ref, wide_ref, product_ref):
    cells, nodes, _ = k_ref.shape
    face = map_ref.shape[1]
    inner = nodes - face
    wide = 2 * face
    eye = lax.broadcasted_iota(jnp.int32, (wide, wide), 0) == lax.broadcasted_iota(jnp.int32, (wide, wide), 1)
    eye = jnp.where(eye[:face], 1.0, 0.0).astype(bf16)
    for c in range(cells):
        select = selection(map_ref[c : c + 1, :])
        both = jnp.concatenate([jnp.zeros((face, face), bf16), select], 1)
        both = jnp.concatenate([eye, both], 0)
        out_ref[c, :, : nodes - wide] = k_ref[c, :, : nodes - wide]
        out_ref[c, :, nodes - wide :] = dot(k_ref[c, :, nodes - wide :], both, ((1,), (1,))).astype(bf16)
        out_ref[c, inner:, :] = dot(select, out_ref[c, inner:, :]).astype(bf16)
        start_ref[c, :inner] = x_ref[c, :inner]
        start_ref[c, inner:] = dot(select, x_ref[c, inner:]).astype(bf16)
        wide_ref[c] = start_ref[c].astype(f32)
        product_ref[c] = dot(out_ref[c], start_ref[c])


def reordered(cell_matrices, states, face_map):
    return pl.pallas_call(
        reorder_kernel,
        in_specs=[vmem()] * 3,
        out_specs=[vmem()] * 4,
        out_shape=[
            jax.ShapeDtypeStruct(cell_matrices.shape, bf16),
            jax.ShapeDtypeStruct(states.shape, bf16),
            jax.ShapeDtypeStruct(states.shape, f32),
            jax.ShapeDtypeStruct(states.shape, f32),
        ],
        compiler_params=SMALL,
        name="reorder",
    )(face_map, cell_matrices, states)


def scatter_rows(part, outs, block, core, place):
    half = outs[0].shape[1]
    rows, cols = outs[0].shape[-2:]
    fine = part.shape[1] // (len(outs) * cols)
    over = 2 * half // fine
    for x in range(part.shape[0] // (rows * over)):
        away = lax.rem(x - place + 4, 4)
        slots = (
            jnp.where(away == 0, 4, jnp.where(away == 1, 6, jnp.where(away == 2, 0, 3))),
            jnp.where(away == 0, 5, jnp.where(away == 1, 1, jnp.where(away == 2, 2, 7))),
        )
        for m, out_ref in enumerate(outs):
            for y in range(2 * half):
                low = (x * over + y % over) * rows
                left = (m * fine + y // over) * cols
                tile = part[low : low + rows, left : left + cols].astype(bf16)
                out_ref[slots[y // half], y % half, block, core] = tile


def pack_kernel(where_ref, now_ref, start_ref, next_ref, own_ref, up_ref, down_ref):
    cells, nodes, _ = now_ref.shape
    face = next_ref.shape[0]
    total = nodes + face
    inner = nodes - face
    half = total // 2
    last_cell = where_ref[3]

    def rows_of(away):
        c = lax.rem(where_ref[0] + away, cells)
        now = now_ref[c]
        after = jnp.where(c == cells - 1, next_ref[...], start_ref[lax.rem(c + 1, cells), :face])
        step = jnp.where(c == last_cell, 0.0, start_ref[c, inner:] - after)
        paired = (now[inner:] - step).astype(bf16)
        return now.astype(bf16), paired

    for away, ref in ((0, own_ref), (1, up_ref), (3, down_ref)):
        now, paired = rows_of(away)
        ref[:nodes] = now
        ref[nodes:total] = paired
    now, paired = rows_of(2)
    up_ref[total:] = now[:half]
    down_ref[total : total + nodes - half] = now[half:]
    down_ref[total + nodes - half :] = paired


def pack(where, now, start, after):
    cells, nodes, orb = now.shape
    total = nodes + after.shape[0]
    sent = jax.ShapeDtypeStruct((total + total // 2, orb), bf16)
    return pl.pallas_call(
        pack_kernel,
        in_specs=[smem()] + [vmem()] * 3,
        out_specs=[vmem()] * 3,
        out_shape=[jax.ShapeDtypeStruct((total, orb), bf16), sent, sent],
        compiler_params=SMALL,
        name="pack",
    )(where, now, start, after)


def collect_kernel(where_ref, own_ref, below_ref, above_ref, low_half_ref, high_half_ref, rows_ref):
    cells, total, _ = rows_ref.shape
    half = total // 2
    place = where_ref[0]
    rows_ref[place] = own_ref[...]
    rows_ref[lax.rem(place + 3, cells)] = below_ref[:total]
    rows_ref[lax.rem(place + 1, cells)] = above_ref[:total]
    far = lax.rem(place + 2, cells)
    rows_ref[far, :half] = low_half_ref[...]
    rows_ref[far, half:] = high_half_ref[...]


def collect(where, own, below, above, low_half, high_half):
    total, orb = own.shape
    return pl.pallas_call(
        collect_kernel,
        in_specs=[smem()] + [vmem()] * 5,
        out_specs=vmem(),
        out_shape=jax.ShapeDtypeStruct((4, total, orb), bf16),
        compiler_params=SMALL,
        name="collect",
    )(where, own, below, above, low_half, high_half)


def right_kernel(where_ref, k_ref, rows_ref, right_ref):
    blocks, total, orb = rows_ref.shape
    nodes = k_ref.shape[1]
    inner = 2 * nodes - total
    is_last = where_ref[1] == 1
    matrix = k_ref[where_ref[0]]
    for s in range(blocks):
        at = slice(s * orb, (s + 1) * orb)
        right_ref[:, at] = dot(matrix, rows_ref[s, :nodes]).astype(bf16)
        at = slice((blocks + s) * orb, (blocks + s + 1) * orb)
        right_ref[:inner, at] = rows_ref[s, :inner]
        paired = rows_ref[s, nodes:]
        right_ref[inner:, at] = jnp.where(is_last, paired, jnp.zeros_like(paired))


def gram_kernel(where_ref, own_ref, other_ref, right_ref, ham_ref, inter_ref, left_ref):
    blocks, total, _ = own_ref.shape
    nodes = right_ref.shape[0]
    inner = 2 * nodes - total
    for ref, core in ((own_ref, where_ref[2]), (other_ref, 1 - where_ref[2])):
        for s in range(blocks):
            left_ref[:inner] = ref[s, :inner]
            left_ref[inner:] = ref[s, nodes:]
            part = dot(left_ref[...], right_ref[...], ((0,), (0,)))
            scatter_rows(part, (ham_ref, inter_ref), s, core, where_ref[4])


def right_of(where, matrices, rows):
    blocks, _, orb = rows.shape
    nodes = matrices.shape[1]
    return pl.pallas_call(
        right_kernel,
        in_specs=[smem(), vmem(), vmem()],
        out_specs=vmem(),
        out_shape=jax.ShapeDtypeStruct((nodes, 2 * blocks * orb), bf16),
        compiler_params=SMALL,
        name="right",
    )(where, matrices, rows)


def gram(where, own, other, right):
    blocks, _, orb = own.shape
    xs, ys, cores = lax.axis_size("x"), lax.axis_size("y"), lax.axis_size("core")
    over = max(1, ys // blocks)
    shape = (2 * xs, ys // 2, blocks, cores, orb // (xs * over), over * blocks * orb // ys)
    return pl.pallas_call(
        gram_kernel,
        in_specs=[smem(), vmem(), vmem(), vmem()],
        out_specs=[vmem(), vmem()],
        out_shape=[jax.ShapeDtypeStruct(shape, bf16)] * 2,
        scratch_shapes=[pltpu.VMEM((right.shape[0], orb), bf16)],
        compiler_params=SMALL,
        name="gram",
    )(where, own, other, right)


def assemble_kernel(scale, pieces_ref, ham_ref, inter_ref):
    ys, xs, cores, _, sub, cols = pieces_ref.shape
    over = ham_ref.shape[0] // (sub * xs)
    for m, out_ref in enumerate((ham_ref, inter_ref)):
        for y in range(ys):
            for c in range(cores):
                for x in range(xs):
                    for k in range(cols // 128):
                        tile = pieces_ref[y, x, c, m, :, k * 128 : (k + 1) * 128]
                        low = (x * over + y % over) * sub
                        left = ((y // over * cols // 128 + k) * cores + c) * 128
                        out_ref[low : low + sub, left : left + 128] = tile.astype(f32) * scale


def assemble(pieces, scale, orb):
    ys, xs, cores, _, sub, cols = pieces.shape
    out = jax.ShapeDtypeStruct((orb, ys * xs * cores * sub * cols // orb), f32)
    return pl.pallas_call(
        lambda *refs: assemble_kernel(scale, *refs),
        in_specs=[vmem()],
        out_specs=[vmem(), vmem()],
        out_shape=[out, out],
        compiler_params=SMALL,
        name="assemble",
    )(pieces)


def summed(parts):
    return jnp.sum(parts.astype(f32), 0).astype(bf16)


def ring(part, axis, step):
    count = lax.axis_size(axis)
    return lax.ppermute(part, axis, [(i, (i + step) % count) for i in range(count)])


def added(*parts):
    return sum(part.astype(f32) for part in parts).astype(bf16)


def x_sum(part):
    below = ring(part[0:2], "x", 1)
    above = ring(part[2:4], "x", -1)
    below_2 = ring(added(below[0], part[6]), "x", 1)
    above_2 = ring(added(above[0], part[7]), "x", -1)
    return jnp.concatenate([added(part[4], above[1], below_2), added(part[5], below[1], above_2)], 0)


def swap_sum(part, axis):
    return summed(lax.all_to_all(part, axis, split_axis=0, concat_axis=0, tiled=True))


def local(cell_matrices, initial_states, face_map):
    face = face_map.shape[1]
    cells_dev, nodes = cell_matrices.shape[:2]
    orb_dev = initial_states.shape[2]
    elems = lax.axis_size(elem)
    zhs, cores, zls = lax.axis_size("zh"), lax.axis_size("core"), lax.axis_size("zl")
    xs, ys = lax.axis_size("x"), lax.axis_size("y")
    head, tail = first_edges(cell_matrices, initial_states, face_map)
    cell_matrices, initial_states, head, tail = lax.optimization_barrier(
        (cell_matrices, initial_states, head, tail)
    )
    above, from_below = neighbours(head, tail)
    matrices, current_b, start, products = reordered(cell_matrices, initial_states, face_map)

    def edges(values):
        return (
            dot(matrices[0, :face], values[0]),
            dot(matrices[-1, -face:], values[-1]),
        )

    previous = start
    current = start
    from_above, next_start, from_below = above[0], above[1], from_below[0]
    for degree in range(PASSES):
        if degree > 0:
            head, tail = edges(current_b)
            from_above, from_below = neighbours(head, tail)
            current_b, head, tail = lax.optimization_barrier((current_b, head, tail))
            products = jnp.einsum("cij,cjo->cio", matrices, current_b, preferred_element_type=f32)
        from_next = jnp.concatenate([products[1:, :face], from_above[None]], 0)
        from_low = jnp.concatenate([from_below[None], products[:-1, -face:]], 0)
        image = jnp.concatenate(
            [
                products[:, :face] + from_low,
                products[:, face:-face],
                products[:, -face:] + from_next,
            ],
            1,
        )
        following = image / filter_width if degree == 0 else 2.0 / filter_width * image - previous
        previous = current
        current = following
        current_b = following.astype(bf16)

    place = lax.axis_index(elem) * cells_dev
    zh = lax.axis_index("zh")
    last_cell = cells_dev * elems - 1 - place
    where = jnp.stack(
        [zh, (zh == last_cell).astype(jnp.int32), lax.axis_index("core"), last_cell, lax.axis_index("x")]
    )

    own, up, down = pack(where, current, start, next_start)
    total = own.shape[0]
    below = ring(up, "zh", 1)
    above = ring(down, "zh", -1)
    low_half = ring(below[total:], "zh", 1)
    high_half = ring(above[total:], "zh", -1)
    rows = collect(where, own, below, above, low_half, high_half)
    other = ring(rows, "core", 1)
    right = right_of(where, matrices, rows)
    parts = gram(where, rows, other, right)
    parts = [swap_sum(x_sum(part), "y") for part in parts]
    part = jnp.stack(parts, 2)
    column = jnp.broadcast_to(part[None], (zls,) + part.shape).reshape((-1,) + part.shape[2:])
    column = lax.all_to_all(column, ("zl", "zh", "core"), split_axis=0, concat_axis=0, tiled=True)
    piece = summed(column.reshape((zls * zhs, cores) + part.shape[2:]))
    pieces = jnp.broadcast_to(piece[None], (ys * xs,) + piece.shape)
    pieces = lax.all_to_all(pieces, ("y", "x"), split_axis=0, concat_axis=0, tiled=True)
    scale = 1.0 / (cells_dev * elems * nodes)
    hamiltonian, intersection = assemble(pieces.reshape((ys, xs) + piece.shape), scale, orb_dev)

    onehot = (face_map[:, :, None] == jnp.arange(face, dtype=jnp.int32)[None, None, :]).astype(bf16)
    upper = jnp.einsum("cfm,cmo->cfo", onehot, current_b[:, -face:], preferred_element_type=f32)
    states = jnp.concatenate([current_b[:, :-face], upper.astype(bf16)], 1)
    return (states, hamiltonian, intersection)


def solution(mesh):
    names = elem + state
    fine = Mesh(mesh.devices.reshape([size for _, size in ELEM + STATE]), names)
    return jax.shard_map(
        local,
        mesh=fine,
        in_specs=(P(elem, None, None), P(elem, None, state), P(elem, None)),
        out_specs=(P(elem, None, state), P(state, None), P(state, None)),
        check_vma=False,
    )
```

```python
import jax
import jax.numpy as jnp
from jax import lax
from jax.experimental import pallas as pl
from jax.experimental.pallas import tpu as pltpu
from jax.sharding import Mesh
from jax.sharding import PartitionSpec as P

PASSES = 4
ELEM = (("y", 8), ("x", 4), ("zl", 3))
STATE = (("zh", 4), ("core", 2))


filter_width = 2.5

f32 = jnp.float32
bf16 = jnp.bfloat16
elem = tuple(name for name, _ in ELEM)
state = tuple(name for name, _ in STATE)


def dot(a, b, dims=((1,), (0,))):
    return lax.dot_general(a, b, (dims, ((), ())), preferred_element_type=f32)


def swapped(odd, even):
    count = lax.axis_size(elem)
    swaps = []
    for first, sent in ((1, odd), (0, even)):
        pairs = [(i, i + 1) for i in range(first, count - 1, 2)]
        swaps.append(lax.ppermute(sent, elem, pairs + [(j, i) for i, j in pairs]))
    return swaps


def neighbours(head, tail):
    even = lax.axis_index(elem) % 2 == 0
    first, second = swapped(jnp.where(even, head, tail), jnp.where(even, tail, head))
    return jnp.where(even, second, first), jnp.where(even, first, second)


def vmem():
    return pl.BlockSpec(memory_space=pltpu.VMEM)


def smem():
    return pl.BlockSpec(memory_space=pltpu.SMEM)


SMALL = pltpu.CompilerParams(vmem_limit_bytes=20 * 1024 * 1024)


def selection(map_row):
    face = map_row.shape[1]
    rows = lax.broadcasted_iota(jnp.int32, (face, face), 0)
    return jnp.where(rows == map_row, 1.0, 0.0).astype(bf16)


def first_edges_kernel(even_ref, map_ref, low_ref, up_ref, first_ref, last_ref, odd_out_ref, even_out_ref):
    face = low_ref.shape[1]
    cells = map_ref.shape[0]
    is_even = even_ref[0] == 1
    head = dot(low_ref[0], first_ref[0])
    up = dot(selection(map_ref[cells - 1 :, :]), up_ref[0]).astype(bf16)
    tail = dot(up, last_ref[0])
    odd_out_ref[0] = jnp.where(is_even, head, tail)
    even_out_ref[0] = jnp.where(is_even, tail, head)
    states = first_ref[0, :face].astype(f32)
    odd_out_ref[1] = states
    even_out_ref[1] = states


def first_edges(is_even, cell_matrices, states, face_map):
    cells, nodes, orb = states.shape
    face = face_map.shape[1]
    out = jax.ShapeDtypeStruct((2, face, orb), f32)
    return pl.pallas_call(
        first_edges_kernel,
        grid=(1,),
        in_specs=[
            smem(),
            pl.BlockSpec((cells, face), lambda i: (0, 0)),
            pl.BlockSpec((1, face, nodes), lambda i: (0, 0, 0)),
            pl.BlockSpec((1, face, nodes), lambda i: (cells - 1, nodes // face - 1, 0)),
            pl.BlockSpec((1, nodes, orb), lambda i: (0, 0, 0)),
            pl.BlockSpec((1, nodes, orb), lambda i: (cells - 1, 0, 0)),
        ],
        out_specs=[pl.BlockSpec((2, face, orb), lambda i: (0, 0, 0))] * 2,
        out_shape=[out, out],
        compiler_params=SMALL,
        name="first_edges",
    )(is_even, face_map, cell_matrices, cell_matrices, states, states)


def first_step_kernel(even_ref, first_ref, second_ref, product_ref, k_ref, wide_ref, now_ref, head_ref, tail_ref, next_ref):
    cells, nodes, _ = product_ref.shape
    face = head_ref.shape[0]
    inner = nodes - face
    is_even = even_ref[0] == 1
    for c in (0, cells - 1, *range(1, cells - 1)):
        if c == 0:
            below = jnp.where(is_even, first_ref[0], second_ref[0])
        else:
            below = product_ref[c - 1, inner:]
        if c == cells - 1:
            above = jnp.where(is_even, second_ref[0], first_ref[0])
        else:
            above = product_ref[c + 1, :face]
        wide_ref[c, :face] = (product_ref[c, :face] + below) / filter_width
        wide_ref[c, face:inner] = product_ref[c, face:inner] / filter_width
        wide_ref[c, inner:] = (product_ref[c, inner:] + above) / filter_width
        now_ref[c] = wide_ref[c].astype(bf16)
    head_ref[...] = dot(k_ref[0, :face], now_ref[0])
    tail_ref[...] = dot(k_ref[cells - 1, inner:], now_ref[cells - 1])
    next_ref[...] = jnp.where(is_even, second_ref[1], first_ref[1])


def first_step(is_even, first, second, products, matrices):
    face = first.shape[1]
    edge = jax.ShapeDtypeStruct((face, products.shape[2]), f32)
    return pl.pallas_call(
        first_step_kernel,
        in_specs=[smem()] + [vmem()] * 4,
        out_specs=[vmem()] * 5,
        out_shape=[products, jax.ShapeDtypeStruct(products.shape, bf16), edge, edge, edge],
        compiler_params=SMALL,
        name="first_step",
    )(is_even, first, second, products, matrices)


def reorder_kernel(map_ref, k_ref, x_ref, out_ref, start_ref, wide_ref, product_ref):
    cells, nodes, _ = k_ref.shape
    face = map_ref.shape[1]
    inner = nodes - face
    wide = 2 * face
    eye = lax.broadcasted_iota(jnp.int32, (wide, wide), 0) == lax.broadcasted_iota(jnp.int32, (wide, wide), 1)
    eye = jnp.where(eye[:face], 1.0, 0.0).astype(bf16)
    for c in range(cells):
        select = selection(map_ref[c : c + 1, :])
        both = jnp.concatenate([jnp.zeros((face, face), bf16), select], 1)
        both = jnp.concatenate([eye, both], 0)
        out_ref[c, :, : nodes - wide] = k_ref[c, :, : nodes - wide]
        out_ref[c, :, nodes - wide :] = dot(k_ref[c, :, nodes - wide :], both, ((1,), (1,))).astype(bf16)
        out_ref[c, inner:, :] = dot(select, out_ref[c, inner:, :]).astype(bf16)
        start_ref[c, :inner] = x_ref[c, :inner]
        start_ref[c, inner:] = dot(select, x_ref[c, inner:]).astype(bf16)
        wide_ref[c] = start_ref[c].astype(f32)
        product_ref[c] = dot(out_ref[c], start_ref[c])


def reordered(cell_matrices, states, face_map):
    return pl.pallas_call(
        reorder_kernel,
        in_specs=[vmem()] * 3,
        out_specs=[vmem()] * 4,
        out_shape=[
            jax.ShapeDtypeStruct(cell_matrices.shape, bf16),
            jax.ShapeDtypeStruct(states.shape, bf16),
            jax.ShapeDtypeStruct(states.shape, f32),
            jax.ShapeDtypeStruct(states.shape, f32),
        ],
        compiler_params=SMALL,
        name="reorder",
    )(face_map, cell_matrices, states)


def scatter_rows(part, out_ref, block, core):
    xs, ys, _, _, rows, cols = out_ref.shape
    for x in range(xs):
        for y in range(ys):
            tile = part[x * rows : (x + 1) * rows, y * cols : (y + 1) * cols].astype(bf16)
            out_ref[x, y, block, core] = tile


def pack_kernel(last_ref, now_ref, start_ref, next_ref, rows_ref):
    cells, nodes, _ = now_ref.shape
    face = next_ref.shape[0]
    inner = nodes - face
    for c in range(cells):
        after = next_ref[...] if c == cells - 1 else start_ref[c + 1, :face]
        step = jnp.where(last_ref[0] == c, 0.0, start_ref[c, inner:] - after)
        rows_ref[c, :nodes] = now_ref[c].astype(bf16)
        rows_ref[c, nodes:] = (now_ref[c, inner:] - step).astype(bf16)


def pack(last_cell, now, start, after):
    cells, nodes, orb = now.shape
    return pl.pallas_call(
        pack_kernel,
        in_specs=[smem()] + [vmem()] * 3,
        out_specs=vmem(),
        out_shape=jax.ShapeDtypeStruct((cells, nodes + after.shape[0], orb), bf16),
        compiler_params=SMALL,
        name="pack",
    )(last_cell, now, start, after)


def right_kernel(where_ref, k_ref, rows_ref, right_ref):
    blocks, total, orb = rows_ref.shape
    nodes = k_ref.shape[1]
    inner = 2 * nodes - total
    is_last = where_ref[1] == 1
    matrix = k_ref[where_ref[0]]
    for s in range(blocks):
        at = slice(s * orb, (s + 1) * orb)
        right_ref[:, at] = dot(matrix, rows_ref[s, :nodes]).astype(bf16)
        at = slice((blocks + s) * orb, (blocks + s + 1) * orb)
        right_ref[:inner, at] = rows_ref[s, :inner]
        paired = rows_ref[s, nodes:]
        right_ref[inner:, at] = jnp.where(is_last, paired, jnp.zeros_like(paired))


def gram_kernel(where_ref, own_ref, other_ref, right_ref, out_ref, left_ref):
    blocks, total, _ = own_ref.shape
    nodes = right_ref.shape[0]
    inner = 2 * nodes - total
    for ref, core in ((own_ref, where_ref[2]), (other_ref, 1 - where_ref[2])):
        for s in range(blocks):
            left_ref[:inner] = ref[s, :inner]
            left_ref[inner:] = ref[s, nodes:]
            part = dot(left_ref[...], right_ref[...], ((0,), (0,)))
            scatter_rows(part, out_ref, s, core)


def right_of(where, matrices, rows):
    blocks, _, orb = rows.shape
    nodes = matrices.shape[1]
    return pl.pallas_call(
        right_kernel,
        in_specs=[smem(), vmem(), vmem()],
        out_specs=vmem(),
        out_shape=jax.ShapeDtypeStruct((nodes, 2 * blocks * orb), bf16),
        compiler_params=SMALL,
        name="right",
    )(where, matrices, rows)


def gram(where, own, other, right):
    blocks, _, orb = own.shape
    xs, ys, cores = lax.axis_size("x"), lax.axis_size("y"), lax.axis_size("core")
    shape = (xs, ys, blocks, cores, orb // xs, 2 * blocks * orb // ys)
    return pl.pallas_call(
        gram_kernel,
        in_specs=[smem(), vmem(), vmem(), vmem()],
        out_specs=vmem(),
        out_shape=jax.ShapeDtypeStruct(shape, bf16),
        scratch_shapes=[pltpu.VMEM((right.shape[0], orb), bf16)],
        compiler_params=SMALL,
        name="gram",
    )(where, own, other, right)


def assemble_kernel(scale, pieces_ref, ham_ref, inter_ref):
    ys, xs, cores, sub, cols = pieces_ref.shape
    orb = sub * xs
    for out_ref, half in ((ham_ref, 0), (inter_ref, 1)):
        for y in range(ys // 2):
            for k in range(cols // orb):
                zh = y * cols // orb + k
                for c in range(cores):
                    for x in range(xs):
                        tile = pieces_ref[half * ys // 2 + y, x, c, :, k * orb : (k + 1) * orb]
                        at = (zh * cores + c) * orb
                        out_ref[x * sub : (x + 1) * sub, at : at + orb] = tile.astype(f32) * scale


def assemble(pieces, scale):
    ys, xs, cores, sub, cols = pieces.shape
    out = jax.ShapeDtypeStruct((sub * xs, ys * cores * cols // 2), f32)
    return pl.pallas_call(
        lambda *refs: assemble_kernel(scale, *refs),
        in_specs=[vmem()],
        out_specs=[vmem(), vmem()],
        out_shape=[out, out],
        compiler_params=SMALL,
        name="assemble",
    )(pieces)


def summed(parts):
    return jnp.sum(parts.astype(f32), 0).astype(bf16)


def ring(part, axis, step):
    count = lax.axis_size(axis)
    return lax.ppermute(part, axis, [(i, (i + step) % count) for i in range(count)])


def swap_sum(part, axis):
    return summed(lax.all_to_all(part, axis, split_axis=0, concat_axis=0, tiled=True))


def local(cell_matrices, initial_states, face_map):
    face = face_map.shape[1]
    cells_dev, nodes = cell_matrices.shape[:2]
    orb_dev = initial_states.shape[2]
    elems = lax.axis_size(elem)
    zhs, cores, zls = lax.axis_size("zh"), lax.axis_size("core"), lax.axis_size("zl")
    xs, ys = lax.axis_size("x"), lax.axis_size("y")
    is_even = (1 - lax.axis_index(elem) % 2).reshape(1)
    sent = first_edges(is_even, cell_matrices, initial_states, face_map)
    cell_matrices, initial_states, *sent = lax.optimization_barrier(
        (cell_matrices, initial_states, *sent)
    )
    first, second = swapped(*sent)
    matrices, current_b, start, products = reordered(cell_matrices, initial_states, face_map)
    previous = start
    current, current_b, head, tail, next_start = first_step(is_even, first, second, products, matrices)
    for degree in range(1, PASSES):
        if degree > 1:
            head = dot(matrices[0, :face], current_b[0])
            tail = dot(matrices[-1, -face:], current_b[-1])
        from_above, from_below = neighbours(head, tail)
        current_b, head, tail = lax.optimization_barrier((current_b, head, tail))
        products = jnp.einsum("cij,cjo->cio", matrices, current_b, preferred_element_type=f32)
        from_next = jnp.concatenate([products[1:, :face], from_above[None]], 0)
        from_low = jnp.concatenate([from_below[None], products[:-1, -face:]], 0)
        image = jnp.concatenate(
            [
                products[:, :face] + from_low,
                products[:, face:-face],
                products[:, -face:] + from_next,
            ],
            1,
        )
        following = 2.0 / filter_width * image - previous
        previous = current
        current = following
        current_b = following.astype(bf16)

    place = lax.axis_index(elem) * cells_dev
    zh = lax.axis_index("zh")
    last_cell = cells_dev * elems - 1 - place
    where = jnp.stack([zh, (zh == last_cell).astype(jnp.int32), lax.axis_index("core")])

    rows = pack(last_cell.reshape(1), current, start, next_start)
    rows = lax.all_to_all(rows, "zh", split_axis=0, concat_axis=0, tiled=True)
    other = ring(rows, "core", 1)
    right = right_of(where, matrices, rows)
    part = gram(where, rows, other, right)
    part = swap_sum(part, "x")
    part = swap_sum(part, "y")
    sub, cols = part.shape[2:]
    column = jnp.broadcast_to(part[None], (zls,) + part.shape).reshape(-1, sub, cols)
    column = lax.all_to_all(column, ("zl", "zh", "core"), split_axis=0, concat_axis=0, tiled=True)
    piece = summed(column.reshape(zls * zhs, cores, sub, cols))
    pieces = jnp.broadcast_to(piece[None], (ys * xs,) + piece.shape)
    pieces = lax.all_to_all(pieces, ("y", "x"), split_axis=0, concat_axis=0, tiled=True)
    scale = 1.0 / (cells_dev * elems * nodes)
    hamiltonian, intersection = assemble(pieces.reshape(ys, xs, cores, sub, cols), scale)

    onehot = (face_map[:, :, None] == jnp.arange(face, dtype=jnp.int32)[None, None, :]).astype(bf16)
    upper = jnp.einsum("cfm,cmo->cfo", onehot, current_b[:, -face:], preferred_element_type=f32)
    states = jnp.concatenate([current_b[:, :-face], upper.astype(bf16)], 1)
    return (states, hamiltonian, intersection)


def solution(mesh):
    names = elem + state
    fine = Mesh(mesh.devices.reshape([size for _, size in ELEM + STATE]), names)
    return jax.shard_map(
        local,
        mesh=fine,
        in_specs=(P(elem, None, None), P(elem, None, state), P(elem, None)),
        out_specs=(P(elem, None, state), P(state, None), P(state, None)),
        check_vma=False,
    )
```

```python
import jax
import jax.numpy as jnp
from jax import lax
from jax.experimental import pallas as pl
from jax.experimental.pallas import tpu as pltpu
from jax.sharding import Mesh
from jax.sharding import PartitionSpec as P

PASSES = 4
ELEM = (("y", 8), ("x", 4), ("zl", 3))
STATE = (("zh", 4), ("core", 2))


filter_width = 2.5

f32 = jnp.float32
bf16 = jnp.bfloat16
elem = tuple(name for name, _ in ELEM)
state = tuple(name for name, _ in STATE)


def dot(a, b, dims=((1,), (0,))):
    return lax.dot_general(a, b, (dims, ((), ())), preferred_element_type=f32)


def swapped(odd, even):
    count = lax.axis_size(elem)
    swaps = []
    for first, sent in ((1, odd), (0, even)):
        pairs = [(i, i + 1) for i in range(first, count - 1, 2)]
        swaps.append(lax.ppermute(sent, elem, pairs + [(j, i) for i, j in pairs]))
    return swaps


def neighbours(head, tail):
    even = lax.axis_index(elem) % 2 == 0
    first, second = swapped(jnp.where(even, head, tail), jnp.where(even, tail, head))
    return jnp.where(even, second, first), jnp.where(even, first, second)


def vmem():
    return pl.BlockSpec(memory_space=pltpu.VMEM)


def smem():
    return pl.BlockSpec(memory_space=pltpu.SMEM)


SMALL = pltpu.CompilerParams(vmem_limit_bytes=20 * 1024 * 1024)


def selection(map_row):
    face = map_row.shape[1]
    rows = lax.broadcasted_iota(jnp.int32, (face, face), 0)
    return jnp.where(rows == map_row, 1.0, 0.0).astype(bf16)


def first_edges_kernel(even_ref, map_ref, low_ref, up_ref, first_ref, last_ref, odd_out_ref, even_out_ref):
    face = low_ref.shape[1]
    cells = map_ref.shape[0]
    is_even = even_ref[0] == 1
    head = dot(low_ref[0], first_ref[0])
    up = dot(selection(map_ref[cells - 1 :, :]), up_ref[0]).astype(bf16)
    tail = dot(up, last_ref[0])
    odd_out_ref[0] = jnp.where(is_even, head, tail)
    even_out_ref[0] = jnp.where(is_even, tail, head)
    states = first_ref[0, :face].astype(f32)
    odd_out_ref[1] = states
    even_out_ref[1] = states


def first_edges(is_even, cell_matrices, states, face_map):
    cells, nodes, orb = states.shape
    face = face_map.shape[1]
    out = jax.ShapeDtypeStruct((2, face, orb), f32)
    return pl.pallas_call(
        first_edges_kernel,
        grid=(1,),
        in_specs=[
            smem(),
            pl.BlockSpec((cells, face), lambda i: (0, 0)),
            pl.BlockSpec((1, face, nodes), lambda i: (0, 0, 0)),
            pl.BlockSpec((1, face, nodes), lambda i: (cells - 1, nodes // face - 1, 0)),
            pl.BlockSpec((1, nodes, orb), lambda i: (0, 0, 0)),
            pl.BlockSpec((1, nodes, orb), lambda i: (cells - 1, 0, 0)),
        ],
        out_specs=[pl.BlockSpec((2, face, orb), lambda i: (0, 0, 0))] * 2,
        out_shape=[out, out],
        name="first_edges",
    )(is_even, face_map, cell_matrices, cell_matrices, states, states)


def first_step_kernel(even_ref, first_ref, second_ref, product_ref, k_ref, wide_ref, now_ref, head_ref, tail_ref, next_ref):
    cells, nodes, _ = product_ref.shape
    face = head_ref.shape[0]
    inner = nodes - face
    is_even = even_ref[0] == 1
    for c in (0, cells - 1, *range(1, cells - 1)):
        if c == 0:
            below = jnp.where(is_even, first_ref[0].astype(f32), second_ref[0].astype(f32))
        else:
            below = product_ref[c - 1, inner:]
        if c == cells - 1:
            above = jnp.where(is_even, second_ref[0].astype(f32), first_ref[0].astype(f32))
        else:
            above = product_ref[c + 1, :face]
        wide_ref[c, :face] = (product_ref[c, :face] + below) / filter_width
        wide_ref[c, face:inner] = product_ref[c, face:inner] / filter_width
        wide_ref[c, inner:] = (product_ref[c, inner:] + above) / filter_width
        now_ref[c] = wide_ref[c].astype(bf16)
    head_ref[...] = dot(k_ref[0, :face], now_ref[0])
    tail_ref[...] = dot(k_ref[cells - 1, inner:], now_ref[cells - 1])
    next_ref[...] = jnp.where(is_even, second_ref[1].astype(f32), first_ref[1].astype(f32))


def first_step(is_even, first, second, products, matrices):
    face = first.shape[1]
    edge = jax.ShapeDtypeStruct((face, products.shape[2]), f32)
    return pl.pallas_call(
        first_step_kernel,
        in_specs=[smem()] + [vmem()] * 4,
        out_specs=[vmem()] * 5,
        out_shape=[products, jax.ShapeDtypeStruct(products.shape, bf16), edge, edge, edge],
        compiler_params=SMALL,
        name="first_step",
    )(is_even, first, second, products, matrices)


def reorder_kernel(map_ref, k_ref, x_ref, out_ref, start_ref, wide_ref, product_ref):
    cells, nodes, _ = k_ref.shape
    face = map_ref.shape[1]
    inner = nodes - face
    wide = 2 * face
    eye = lax.broadcasted_iota(jnp.int32, (wide, wide), 0) == lax.broadcasted_iota(jnp.int32, (wide, wide), 1)
    eye = jnp.where(eye[:face], 1.0, 0.0).astype(bf16)
    for c in range(cells):
        select = selection(map_ref[c : c + 1, :])
        both = jnp.concatenate([jnp.zeros((face, face), bf16), select], 1)
        both = jnp.concatenate([eye, both], 0)
        out_ref[c, :, : nodes - wide] = k_ref[c, :, : nodes - wide]
        out_ref[c, :, nodes - wide :] = dot(k_ref[c, :, nodes - wide :], both, ((1,), (1,))).astype(bf16)
        out_ref[c, inner:, :] = dot(select, out_ref[c, inner:, :]).astype(bf16)
        start_ref[c, :inner] = x_ref[c, :inner]
        start_ref[c, inner:] = dot(select, x_ref[c, inner:]).astype(bf16)
        wide_ref[c] = start_ref[c].astype(f32)
        product_ref[c] = dot(out_ref[c], start_ref[c])


def reordered(cell_matrices, states, face_map):
    return pl.pallas_call(
        reorder_kernel,
        in_specs=[vmem()] * 3,
        out_specs=[vmem()] * 4,
        out_shape=[
            jax.ShapeDtypeStruct(cell_matrices.shape, bf16),
            jax.ShapeDtypeStruct(states.shape, bf16),
            jax.ShapeDtypeStruct(states.shape, f32),
            jax.ShapeDtypeStruct(states.shape, f32),
        ],
        compiler_params=SMALL,
        name="reorder",
    )(face_map, cell_matrices, states)


def scatter_rows(part, out_ref, block, core):
    xs, ys, _, _, rows, cols = out_ref.shape
    for x in range(xs):
        for y in range(ys):
            tile = part[x * rows : (x + 1) * rows, y * cols : (y + 1) * cols].astype(bf16)
            out_ref[x, y, block, core] = tile


def pack_kernel(last_ref, now_ref, start_ref, next_ref, rows_ref):
    cells, nodes, _ = now_ref.shape
    face = next_ref.shape[0]
    inner = nodes - face
    for c in range(cells):
        after = next_ref[...] if c == cells - 1 else start_ref[c + 1, :face]
        step = jnp.where(last_ref[0] == c, 0.0, start_ref[c, inner:] - after)
        rows_ref[c, :nodes] = now_ref[c].astype(bf16)
        rows_ref[c, nodes:] = (now_ref[c, inner:] - step).astype(bf16)


def pack(last_cell, now, start, after):
    cells, nodes, orb = now.shape
    return pl.pallas_call(
        pack_kernel,
        in_specs=[smem()] + [vmem()] * 3,
        out_specs=vmem(),
        out_shape=jax.ShapeDtypeStruct((cells, nodes + after.shape[0], orb), bf16),
        compiler_params=SMALL,
        name="pack",
    )(last_cell, now, start, after)


def right_kernel(where_ref, k_ref, rows_ref, right_ref):
    blocks, total, orb = rows_ref.shape
    nodes = k_ref.shape[1]
    inner = 2 * nodes - total
    is_last = where_ref[1] == 1
    matrix = k_ref[where_ref[0]]
    for s in range(blocks):
        at = slice(s * orb, (s + 1) * orb)
        right_ref[:, at] = dot(matrix, rows_ref[s, :nodes]).astype(bf16)
        at = slice((blocks + s) * orb, (blocks + s + 1) * orb)
        right_ref[:inner, at] = rows_ref[s, :inner]
        paired = rows_ref[s, nodes:]
        right_ref[inner:, at] = jnp.where(is_last, paired, jnp.zeros_like(paired))


def gram_kernel(where_ref, own_ref, other_ref, right_ref, out_ref, left_ref):
    blocks, total, _ = own_ref.shape
    nodes = right_ref.shape[0]
    inner = 2 * nodes - total
    for ref, core in ((own_ref, where_ref[2]), (other_ref, 1 - where_ref[2])):
        for s in range(blocks):
            left_ref[:inner] = ref[s, :inner]
            left_ref[inner:] = ref[s, nodes:]
            part = dot(left_ref[...], right_ref[...], ((0,), (0,)))
            scatter_rows(part, out_ref, s, core)


def right_of(where, matrices, rows):
    blocks, _, orb = rows.shape
    nodes = matrices.shape[1]
    return pl.pallas_call(
        right_kernel,
        in_specs=[smem(), vmem(), vmem()],
        out_specs=vmem(),
        out_shape=jax.ShapeDtypeStruct((nodes, 2 * blocks * orb), bf16),
        compiler_params=SMALL,
        name="right",
    )(where, matrices, rows)


def gram(where, own, other, right):
    blocks, _, orb = own.shape
    xs, ys, cores = lax.axis_size("x"), lax.axis_size("y"), lax.axis_size("core")
    shape = (xs, ys, blocks, cores, orb // xs, 2 * blocks * orb // ys)
    return pl.pallas_call(
        gram_kernel,
        in_specs=[smem(), vmem(), vmem(), vmem()],
        out_specs=vmem(),
        out_shape=jax.ShapeDtypeStruct(shape, bf16),
        scratch_shapes=[pltpu.VMEM((right.shape[0], orb), bf16)],
        compiler_params=SMALL,
        name="gram",
    )(where, own, other, right)


def assemble_kernel(scale, pieces_ref, ham_ref, inter_ref):
    ys, xs, cores, sub, cols = pieces_ref.shape
    orb = sub * xs
    for out_ref, half in ((ham_ref, 0), (inter_ref, 1)):
        for y in range(ys // 2):
            for k in range(cols // orb):
                zh = y * cols // orb + k
                for c in range(cores):
                    for x in range(xs):
                        tile = pieces_ref[half * ys // 2 + y, x, c, :, k * orb : (k + 1) * orb]
                        at = (zh * cores + c) * orb
                        out_ref[x * sub : (x + 1) * sub, at : at + orb] = tile.astype(f32) * scale


def assemble(pieces, scale):
    ys, xs, cores, sub, cols = pieces.shape
    out = jax.ShapeDtypeStruct((sub * xs, ys * cores * cols // 2), f32)
    return pl.pallas_call(
        lambda *refs: assemble_kernel(scale, *refs),
        in_specs=[vmem()],
        out_specs=[vmem(), vmem()],
        out_shape=[out, out],
        compiler_params=SMALL,
        name="assemble",
    )(pieces)


def summed(parts):
    return jnp.sum(parts.astype(f32), 0).astype(bf16)


def ring(part, axis, step):
    count = lax.axis_size(axis)
    return lax.ppermute(part, axis, [(i, (i + step) % count) for i in range(count)])


def swap_sum(part, axis):
    return summed(lax.all_to_all(part, axis, split_axis=0, concat_axis=0, tiled=True))


def local(cell_matrices, initial_states, face_map):
    face = face_map.shape[1]
    cells_dev, nodes = cell_matrices.shape[:2]
    orb_dev = initial_states.shape[2]
    elems = lax.axis_size(elem)
    zhs, cores, zls = lax.axis_size("zh"), lax.axis_size("core"), lax.axis_size("zl")
    xs, ys = lax.axis_size("x"), lax.axis_size("y")
    is_even = (1 - lax.axis_index(elem) % 2).reshape(1)
    sent = first_edges(is_even, cell_matrices, initial_states, face_map)
    cell_matrices, initial_states, *sent = lax.optimization_barrier(
        (cell_matrices, initial_states, *sent)
    )
    first, second = swapped(*sent)
    matrices, current_b, start, products = reordered(cell_matrices, initial_states, face_map)
    previous = start
    current, current_b, head, tail, next_start = first_step(is_even, first, second, products, matrices)
    for degree in range(1, PASSES):
        if degree > 1:
            head = dot(matrices[0, :face], current_b[0])
            tail = dot(matrices[-1, -face:], current_b[-1])
        from_above, from_below = neighbours(head, tail)
        current_b, head, tail = lax.optimization_barrier((current_b, head, tail))
        products = jnp.einsum("cij,cjo->cio", matrices, current_b, preferred_element_type=f32)
        from_next = jnp.concatenate([products[1:, :face], from_above[None]], 0)
        from_low = jnp.concatenate([from_below[None], products[:-1, -face:]], 0)
        image = jnp.concatenate(
            [
                products[:, :face] + from_low,
                products[:, face:-face],
                products[:, -face:] + from_next,
            ],
            1,
        )
        following = 2.0 / filter_width * image - previous
        previous = current
        current = following
        current_b = following.astype(bf16)

    place = lax.axis_index(elem) * cells_dev
    zh = lax.axis_index("zh")
    last_cell = cells_dev * elems - 1 - place
    where = jnp.stack([zh, (zh == last_cell).astype(jnp.int32), lax.axis_index("core")])

    rows = pack(last_cell.reshape(1), current, start, next_start)
    rows = lax.all_to_all(rows, "zh", split_axis=0, concat_axis=0, tiled=True)
    other = ring(rows, "core", 1)
    right = right_of(where, matrices, rows)
    part = gram(where, rows, other, right)
    part = swap_sum(part, "x")
    part = swap_sum(part, "y")
    sub, cols = part.shape[2:]
    column = jnp.broadcast_to(part[None], (zls,) + part.shape).reshape(-1, sub, cols)
    column = lax.all_to_all(column, ("zl", "zh", "core"), split_axis=0, concat_axis=0, tiled=True)
    piece = summed(column.reshape(zls * zhs, cores, sub, cols))
    pieces = jnp.broadcast_to(piece[None], (ys * xs,) + piece.shape)
    pieces = lax.all_to_all(pieces, ("y", "x"), split_axis=0, concat_axis=0, tiled=True)
    scale = 1.0 / (cells_dev * elems * nodes)
    hamiltonian, intersection = assemble(pieces.reshape(ys, xs, cores, sub, cols), scale)

    onehot = (face_map[:, :, None] == jnp.arange(face, dtype=jnp.int32)[None, None, :]).astype(bf16)
    upper = jnp.einsum("cfm,cmo->cfo", onehot, current_b[:, -face:], preferred_element_type=f32)
    states = jnp.concatenate([current_b[:, :-face], upper.astype(bf16)], 1)
    return (states, hamiltonian, intersection)


def solution(mesh):
    names = elem + state
    fine = Mesh(mesh.devices.reshape([size for _, size in ELEM + STATE]), names)
    return jax.shard_map(
        local,
        mesh=fine,
        in_specs=(P(elem, None, None), P(elem, None, state), P(elem, None)),
        out_specs=(P(elem, None, state), P(state, None), P(state, None)),
        check_vma=False,
    )
```
